32 devices in a mesh: dp: 4 (over z), row: 2 (over y), col: 4 (over x, core).
Axes of the slice: x: 2, y: 2, z: 4, core: 2. Of those that a mesh axis runs over, the one named last changes fastest.
Arguments:
- hidden_in: bfloat16 [1024, 2048], P('dp', ('row', 'col')), may hold values from -6 to 6
- seq_lengths: int32 [4], P('dp'), may hold values from 128 to 256, as said below
- query_weight: bfloat16 [2048, 2048], P('row', 'col'), may hold values from -0.8838835 to 0.8838835
- key_weight: bfloat16 [2048, 2048], P('row', 'col'), may hold values from -0.8838835 to 0.8838835
- value_weight: bfloat16 [2048, 2048], P('row', 'col'), may hold values from -0.125 to 0.125
- output_weight: bfloat16 [2048, 2048], P('col', 'row'), may hold values from -0.125 to 0.125
- gate_weight: bfloat16 [2048, 8192], P('row', 'col'), may hold values from -0.125 to 0.125
- up_weight: bfloat16 [2048, 8192], P('row', 'col'), may hold values from -0.125 to 0.125
- down_weight: bfloat16 [8192, 2048], P('col', 'row'), may hold values from -0.0625 to 0.0625
- query_gain: float32 [2048], replicated, may hold values from 0.5 to 5
- key_gain: float32 [2048], replicated, may hold values from 0.5 to 5
- mixer_gain: float32 [2048], replicated, may hold values from 0.1 to 1.9
- feed_gain: float32 [2048], replicated, may hold values from 0.1 to 1.9
- out_grad: bfloat16 [1024, 2048], P('dp', ('row', 'col')), may hold values from -6 to 6
Outputs:
- block_out: bfloat16 [1024, 2048], P('dp', ('row', 'col'))
- input_grad: bfloat16 [1024, 2048], P('dp', ('row', 'col'))
- query_weight_grad: float32 [2048, 2048], P(('row', 'dp'), 'col')
- key_weight_grad: float32 [2048, 2048], P(('row', 'dp'), 'col')
- value_weight_grad: float32 [2048, 2048], P(('row', 'dp'), 'col')
- output_weight_grad: float32 [2048, 2048], P(('col', 'dp'), 'row')
- gate_weight_grad: float32 [2048, 8192], P(('row', 'dp'), 'col')
- up_weight_grad: float32 [2048, 8192], P(('row', 'dp'), 'col')
- down_weight_grad: float32 [8192, 2048], P(('col', 'dp'), 'row')
- query_gain_grad: float32 [2048], replicated
- key_gain_grad: float32 [2048], replicated
- mixer_gain_grad: float32 [2048], replicated
- feed_gain_grad: float32 [2048], replicated
The draws below stay inside these ranges and needn't reach their ends.
Inputs may be any that keep to these rules, and one draw needn't show every extreme that they name: `seq_lengths`: each index of dp holds one sequence in its first slots; the other slots are padding.
All inputs are finite; a program needn't handle non-finite values.
Results may differ from the reference program's by a relative error of at most 0.015.
Values may be sent and summed in bfloat16 or wider, within the bound.
No kernel may reach another device: no remote copies, remote signals or barrier semaphores. Data moves between devices by JAX's collectives and lax.ppermute only.
A program may use at most 192 MiB of HBM per device.

```python
import jax
import jax.numpy as jnp
from jax import lax

D = 2048
FF = 8192
HEADS = 16
HD = 128
TOK_DEV = 256
MIN_LEN = 128
DOCS = 4
TOKENS = 1024


def draw_seq_lengths(key, part):
    key_len, key_top, key_low = jax.random.split(jax.random.fold_in(key, 7), 3)
    lengths = jax.random.randint(key_len, (DOCS,), MIN_LEN, TOK_DEV + 1)
    longest = jax.random.randint(key_top, (), 0, DOCS)
    shortest = (longest + 1 + jax.random.randint(key_low, (), 0, DOCS - 1)) % DOCS
    lengths = lengths.at[shortest].set(MIN_LEN).at[longest].set(TOK_DEV)
    return lengths.astype(jnp.int32)


def gain_values(seed_key):
    return jax.random.uniform(seed_key, (D,), jnp.float32, 0.5, 1.5)


def draw_query_gain(key, part):
    return gain_values(jax.random.fold_in(key, 11))


def draw_key_gain(key, part):
    return gain_values(jax.random.fold_in(key, 23))


def projection_pair(key):
    base_key = jax.random.fold_in(key, 31)
    key_query, key_key = jax.random.split(base_key, 2)
    scale = D ** (-0.5)
    query_part = jax.random.truncated_normal(key_query, -6.0, 6.0, (D, D), jnp.float32) * scale
    key_part = jax.random.truncated_normal(key_key, -6.0, 6.0, (D, D), jnp.float32) * scale
    return (query_part, key_part)


def draw_query_weight(key, part):
    return projection_pair(key)[0].astype(jnp.bfloat16)


def draw_key_weight(key, part):
    return projection_pair(key)[1].astype(jnp.bfloat16)


def block_scale(rng, shape, cuts, least, top_value):
    def one(dim, blocks):
        steps = jax.random.uniform(jax.random.fold_in(jax.random.fold_in(rng, 6), dim), (blocks,), jnp.float32, least / len(cuts), top_value / len(cuts))
        return jnp.repeat(jnp.exp(steps), shape[dim] // blocks).reshape((-1,) + (1,) * (len(shape) - dim - 1))

    gain = one(*cuts[0])
    for cut in cuts[1:]:
        gain = gain * one(*cut)
    return gain


def bell_draw(key, dims, spread, limit, cuts=(), kind=jnp.bfloat16):
    drawn = jax.random.normal(key, dims, jnp.float32) * spread
    if len(cuts) > 0:
        drawn = block_scale(key, dims, cuts, -0.22, 0.18) * drawn
    return jnp.clip(drawn, min=-limit, max=limit).astype(kind)


def setup_inputs(seed: int = 0) -> dict:
    key_list = jax.random.split(jax.random.key(seed), 15)
    hidden_in = bell_draw(key_list[0], (TOKENS, D), 1.0, 6.0, ((0, 4), (1, 8)))
    seq_lengths = draw_seq_lengths(jax.random.fold_in(key_list[14], 71), 0)
    query_weight = draw_query_weight(jax.random.fold_in(key_list[14], 71), 0)
    key_weight = draw_key_weight(jax.random.fold_in(key_list[14], 71), 0)
    value_weight = bell_draw(key_list[4], (D, D), D ** -0.5, 0.125, ((0, 2), (1, 4)))
    output_weight = bell_draw(key_list[5], (D, D), D ** -0.5, 0.125, ((0, 4), (1, 2)))
    gate_weight = bell_draw(key_list[6], (D, FF), D ** -0.5, 0.125, ((0, 2), (1, 4)))
    up_weight = bell_draw(key_list[7], (D, FF), D ** -0.5, 0.125, ((0, 2), (1, 4)))
    down_weight = bell_draw(key_list[8], (FF, D), FF ** -0.5, 0.0625, ((0, 4), (1, 2)))
    query_gain = draw_query_gain(jax.random.fold_in(key_list[14], 71), 0)
    key_gain = draw_key_gain(jax.random.fold_in(key_list[14], 71), 0)
    mixer_gain = jnp.clip(1.0 + 0.18 * jax.random.normal(key_list[11], (D,), jnp.float32), 0.1, 1.9)
    feed_gain = jnp.clip(1.0 + 0.18 * jax.random.normal(key_list[12], (D,), jnp.float32), 0.1, 1.9)
    out_grad = bell_draw(key_list[13], (TOKENS, D), 1.0, 6.0, ((0, 4), (1, 8)))
    return dict(hidden_in=hidden_in, seq_lengths=seq_lengths, query_weight=query_weight, key_weight=key_weight, value_weight=value_weight, output_weight=output_weight, gate_weight=gate_weight, up_weight=up_weight, down_weight=down_weight, query_gain=query_gain, key_gain=key_gain, mixer_gain=mixer_gain, feed_gain=feed_gain, out_grad=out_grad)


epsilon = 1e-06
rope_base = 500000.0

@jax.custom_vjp
def low(v):
    return lax.optimization_barrier(v.astype(jnp.bfloat16)).astype(jnp.float32)

@jax.custom_vjp
def low_back(v):
    return v

def low_keep(v):
    return (low(v), None)

def low_pass(kept, grad):
    return (grad,)

def back_keep(v):
    return (v, None)

def back_low(kept, grad):
    return (low(grad),)
low.defvjp(low_keep, low_pass)
low_back.defvjp(back_keep, back_low)

def matmul(left, right):
    return jnp.dot(left, right, precision=lax.Precision.HIGHEST, preferred_element_type=jnp.float32)

def rms_scale(tensor):
    return lax.rsqrt(lax.optimization_barrier(jnp.mean(tensor * tensor, axis=-1, keepdims=True)) + epsilon)

def rope_tables():
    positions = jnp.arange(TOK_DEV, dtype=jnp.float32)
    rates = rope_base ** (-2.0 * jnp.arange(HD // 2, dtype=jnp.float32) / HD)
    angles = positions[:, None] * rates[None, :]
    return (jnp.cos(angles)[:, None, :], jnp.sin(angles)[:, None, :])

def rotate(tensor, cosine, sine):
    half_dim = tensor.shape[-1] // 2
    first_half = tensor[..., :half_dim]
    second_half = tensor[..., half_dim:]
    return jnp.concatenate([first_half * cosine - second_half * sine, second_half * cosine + first_half * sine], -1)

def attend_one(packed):
    queries, keys, values, seq_length = packed
    scores = jnp.einsum('qhd,khd->hqk', queries, keys, precision=lax.Precision.HIGHEST) * HD ** (-0.5)
    scores = low_back(scores)
    query_pos = jnp.arange(TOK_DEV)[:, None]
    key_pos = jnp.arange(TOK_DEV)[None, :]
    allowed = (key_pos <= query_pos) & (key_pos < seq_length)
    scores = jnp.where(allowed[None], scores, -1e+30)
    row_max = lax.optimization_barrier(jnp.max(scores, axis=-1, keepdims=True))
    exponent = jnp.exp(scores - row_max)
    probability = exponent / lax.optimization_barrier(jnp.sum(exponent, axis=-1, keepdims=True))
    return jnp.einsum('hqk,khd->qhd', low(probability), values, precision=lax.Precision.HIGHEST)

def forward(hidden, query_weight, key_weight, value_weight, output_weight, gate_weight, up_weight, down_weight, query_gain, key_gain, mixer_gain, feed_gain, seq_lengths):
    query = low_back(matmul(hidden, query_weight))
    key_proj = low_back(matmul(hidden, key_weight))
    value_proj = low_back(matmul(hidden, value_weight))
    query_norm = query * rms_scale(query) * query_gain
    key_norm = key_proj * rms_scale(key_proj) * key_gain
    cosine, sine = rope_tables()
    shaped = (DOCS, TOK_DEV, HEADS, HD)
    query_rot = low(rotate(query_norm.reshape(shaped), cosine, sine))
    key_rot = low(rotate(key_norm.reshape(shaped), cosine, sine))
    value_low = low(value_proj.reshape(shaped))
    attended = lax.map(jax.checkpoint(attend_one), (query_rot, key_rot, value_low, seq_lengths))
    attended = low_back(low(attended.reshape(TOKENS, D)))
    mixer_out = low_back(matmul(attended, output_weight))
    residual = hidden + mixer_out * rms_scale(mixer_out) * mixer_gain
    residual_low = low(residual)
    gate_val = low_back(matmul(residual_low, gate_weight))
    up_val = low_back(matmul(residual_low, up_weight))
    hidden_low = low(jax.nn.silu(gate_val) * up_val)
    feed_out = low_back(matmul(hidden_low, down_weight))
    return residual + feed_out * rms_scale(feed_out) * feed_gain

def reference(hidden_in, seq_lengths, query_weight, key_weight, value_weight, output_weight, gate_weight, up_weight, down_weight, query_gain, key_gain, mixer_gain, feed_gain, out_grad):

    def closed(*params):
        return forward(*params, seq_lengths)
    outputs, pullback = jax.vjp(closed, hidden_in.astype(jnp.float32), query_weight.astype(jnp.float32), key_weight.astype(jnp.float32), value_weight.astype(jnp.float32), output_weight.astype(jnp.float32), gate_weight.astype(jnp.float32), up_weight.astype(jnp.float32), down_weight.astype(jnp.float32), query_gain.astype(jnp.float32), key_gain.astype(jnp.float32), mixer_gain.astype(jnp.float32), feed_gain.astype(jnp.float32))
    slots = jnp.arange(TOKENS, dtype=jnp.int32)
    owner = slots // TOK_DEV
    valid = slots % TOK_DEV < seq_lengths[owner]
    grads = pullback(jnp.where(valid[:, None], out_grad.astype(jnp.float32), 0.0))
    return (outputs.astype(jnp.bfloat16), grads[0].astype(jnp.bfloat16), grads[1], grads[2], grads[3], grads[4], grads[5], grads[6], grads[7], grads[8], grads[9], grads[10], grads[11])
```

```python
import jax
import jax.numpy as jnp
from jax import lax
from jax.sharding import PartitionSpec as P

D = 2048
HD = 128

epsilon = 1e-06
rope_base = 500000.0

BF = jnp.bfloat16
F32 = jnp.float32


def mul_f32(left, right):
    return jnp.dot(left, right, preferred_element_type=F32)


def across_rows(left, right):
    return lax.dot_general(left, right, (((0,), (0,)), ((), ())), preferred_element_type=F32)


def against_cols(left, right):
    return lax.dot_general(left, right, (((1,), (1,)), ((), ())), preferred_element_type=F32)


def swap(tensor, axis, bit):
    size = lax.axis_size(axis)
    return lax.ppermute(tensor, axis, [(i, i ^ bit) for i in range(size)])


def bits_of(axis):
    size = lax.axis_size(axis)
    bits = []
    bit = 1
    while bit < size:
        bits.append(bit)
        bit *= 2
    return bits


def ordered(pieces, axis, dim):
    me = lax.axis_index(axis)
    for bit in bits_of(axis):
        flip = (me & bit) != 0
        moved = list(pieces)
        for j in range(len(pieces)):
            if not j & bit:
                moved[j] = jnp.where(flip, pieces[j | bit], pieces[j])
                moved[j | bit] = jnp.where(flip, pieces[j], pieces[j | bit])
        pieces = moved
    return jnp.concatenate(pieces, dim)


def gather_pieces(tensor, axis, dim):
    pieces = {0: tensor}
    width = tensor.shape[dim]
    for bit in reversed(bits_of(axis)):
        keys = sorted(pieces)
        packed = jnp.concatenate([pieces[k] for k in keys], dim) if len(keys) > 1 else pieces[0]
        got = swap(packed, axis, bit)
        for place, k in enumerate(keys):
            pieces[k | bit] = lax.slice_in_dim(got, place * width, (place + 1) * width, axis=dim)
    return [pieces[j] for j in range(lax.axis_size(axis))]


def gather(tensor, axis, dim=1):
    return ordered(gather_pieces(tensor, axis, dim), axis, dim)


def share(tensor, index, width):
    return lax.dynamic_slice_in_dim(tensor, index * width, width, 1)


def scatter_sum(tensor, axis, kind=BF):
    size = lax.axis_size(axis)
    me = lax.axis_index(axis)
    width = tensor.shape[1] // size
    held = {j: share(tensor, me ^ j, width) for j in range(size)}
    for bit in bits_of(axis):
        away = [j for j in sorted(held) if j & bit]
        packed = jnp.concatenate([held[j].astype(kind) for j in away], 1)
        got = swap(packed, axis, bit)
        for place, j in enumerate(away):
            part = lax.slice_in_dim(got, place * width, (place + 1) * width, axis=1)
            held[j ^ bit] = held[j ^ bit] + part.astype(F32)
            del held[j]
    return held[0]


def total(tensor):
    for axis in ("col", "row"):
        for bit in bits_of(axis):
            tensor = tensor + swap(tensor, axis, bit)
    return tensor


def dp_share(tensor):
    return lax.all_to_all(tensor, "dp", 1, 0, tiled=True)


def dp_whole(tensor):
    size = lax.axis_size("dp")
    spread = jnp.broadcast_to(tensor[None], (size,) + tensor.shape)
    got = lax.all_to_all(spread, "dp", 0, 0, tiled=True)
    return got.reshape((size * tensor.shape[0], tensor.shape[1]))


def rope_tables(row_count):
    positions = jnp.arange(row_count, dtype=F32)
    rates = rope_base ** (-2.0 * jnp.arange(HD // 2, dtype=F32) / HD)
    angles = positions[:, None] * rates[None, :]
    return (jnp.cos(angles), jnp.sin(angles))


def rotate(tensor, cosine, sine):
    half = HD // 2
    parts = []
    for start in range(0, tensor.shape[1], HD):
        first = tensor[:, start : start + half]
        second = tensor[:, start + half : start + HD]
        parts.append(first * cosine - second * sine)
        parts.append(second * cosine + first * sine)
    return jnp.concatenate(parts, 1)


def heads_of(tensor):
    return [tensor[:, s : s + HD] for s in range(0, tensor.shape[1], HD)]


def attend_forward(queries, keys, values, seq_length):
    count = queries.shape[0]
    query_pos = jnp.arange(count)[:, None]
    key_pos = jnp.arange(count)[None, :]
    allowed = (key_pos <= query_pos) & (key_pos < seq_length)
    outputs, probs = [], []
    for q, k, v in zip(heads_of(queries), heads_of(keys), heads_of(values)):
        scores = jnp.where(allowed, against_cols(q, k) * HD ** (-0.5), -1e30)
        row_max = jnp.max(scores, axis=-1, keepdims=True)
        exponent = jnp.exp(scores - row_max)
        p = exponent / jnp.sum(exponent, axis=-1, keepdims=True)
        probs.append(p)
        outputs.append(mul_f32(p.astype(BF), v))
    return jnp.concatenate(outputs, 1), probs


def attend_backward(queries, keys, values, grad_attended, probs):
    scale = HD ** (-0.5)
    gq, gk, gv = [], [], []
    for q, k, v, g, p in zip(
        heads_of(queries), heads_of(keys), heads_of(values), heads_of(grad_attended), probs
    ):
        grad_prob = against_cols(g, v)
        centre = jnp.sum(p * grad_prob, axis=-1, keepdims=True)
        grad_scores = (p * (grad_prob - centre)).astype(BF)
        gq.append(mul_f32(grad_scores, k) * scale)
        gk.append(across_rows(grad_scores, q) * scale)
        gv.append(across_rows(p.astype(BF), g))
    return jnp.concatenate(gq, 1), jnp.concatenate(gk, 1), jnp.concatenate(gv, 1)


def norm_backward(grad_norm, source, scale_rows, gain_part, stat_sum):
    weighted = grad_norm * gain_part
    return scale_rows * weighted - source * scale_rows**3 * stat_sum[:, None] / D


def place_gain(term, offset):
    return lax.dynamic_update_slice_in_dim(jnp.zeros((D,), F32), term, offset, 0)


def body(
    hidden_in,
    seq_lengths,
    query_weight,
    key_weight,
    value_weight,
    output_weight,
    gate_weight,
    up_weight,
    down_weight,
    query_gain,
    key_gain,
    mixer_gain,
    feed_gain,
    out_grad,
):
    row_count, width = hidden_in.shape
    row_place = lax.axis_index("row")
    col_place = lax.axis_index("col")
    col_size = lax.axis_size("col")
    feature_start = (row_place * col_size + col_place) * width
    block_start = row_place * col_size * width
    block_width = col_size * width
    head_start = (col_place * lax.axis_size("row") + row_place) * width
    query_gain_part = lax.dynamic_slice_in_dim(query_gain, head_start, width)
    key_gain_part = lax.dynamic_slice_in_dim(key_gain, head_start, width)
    mixer_gain_part = lax.dynamic_slice_in_dim(mixer_gain, feature_start, width)
    feed_gain_part = lax.dynamic_slice_in_dim(feed_gain, feature_start, width)
    mixer_gain_block = lax.dynamic_slice_in_dim(mixer_gain, block_start, block_width)
    feed_gain_block = lax.dynamic_slice_in_dim(feed_gain, block_start, block_width)
    seq_length = seq_lengths[0]
    cosine, sine = rope_tables(row_count)

    input_block = gather(hidden_in, "col")
    query_part = mul_f32(input_block, query_weight)
    key_part = mul_f32(input_block, key_weight)
    value_part = mul_f32(input_block, value_weight)
    query = scatter_sum(query_part, "row", F32)
    key_proj = scatter_sum(key_part, "row", F32)
    value_low = scatter_sum(value_part, "row").astype(BF)
    square_sums = total(jnp.stack([jnp.sum(query * query, 1), jnp.sum(key_proj * key_proj, 1)]))
    query_scale = lax.rsqrt(square_sums[0] / D + epsilon)[:, None]
    key_scale = lax.rsqrt(square_sums[1] / D + epsilon)[:, None]
    query_rot = rotate(query * query_scale * query_gain_part, cosine, sine).astype(BF)
    key_rot = rotate(key_proj * key_scale * key_gain_part, cosine, sine).astype(BF)
    attended, probs = attend_forward(query_rot, key_rot, value_low, seq_length)
    attended_rows = gather(attended.astype(BF), "row")
    mixer_out = scatter_sum(mul_f32(attended_rows, output_weight), "col")
    mixer_block = gather(mixer_out.astype(BF), "col").astype(F32)
    mixer_scale = lax.rsqrt(total(jnp.sum(mixer_out * mixer_out, 1)) / D + epsilon)[:, None]
    residual = hidden_in.astype(F32) + mixer_out * mixer_scale * mixer_gain_part
    residual_block = (
        input_block.astype(F32) + mixer_block * mixer_scale * mixer_gain_block
    ).astype(BF)

    gate_val = scatter_sum(mul_f32(residual_block, gate_weight), "row")
    up_val = scatter_sum(mul_f32(residual_block, up_weight), "row")
    sigmoid_val = jax.nn.sigmoid(gate_val)
    activated = gate_val * sigmoid_val
    hidden_low = (activated * up_val).astype(BF)
    hidden_rows = gather(hidden_low, "row")
    feed_out = scatter_sum(mul_f32(hidden_rows, down_weight), "col")
    feed_block = gather(feed_out.astype(BF), "col").astype(F32)

    valid = (jnp.arange(row_count) < seq_length)[:, None]
    grad_block = jnp.where(valid, gather(out_grad, "col").astype(F32), 0.0)
    grad_out = jnp.where(valid, out_grad.astype(F32), 0.0)
    feed_sums = total(
        jnp.stack(
            [jnp.sum(feed_out * feed_out, 1), jnp.sum(grad_out * feed_gain_part * feed_out, 1)]
        )
    )
    feed_scale = lax.rsqrt(feed_sums[0] / D + epsilon)[:, None]
    block_out = (residual + feed_out * feed_scale * feed_gain_part).astype(BF)
    feed_gain_term = jnp.sum(grad_out * feed_out * feed_scale, 0)
    grad_feed = norm_backward(grad_out, feed_out, feed_scale, feed_gain_part, feed_sums[1])
    grad_feed_block = norm_backward(
        grad_block, feed_block, feed_scale, feed_gain_block, feed_sums[1]
    ).astype(BF)

    grad_hidden = scatter_sum(against_cols(grad_feed_block, down_weight), "row")
    grad_gate = (
        grad_hidden * up_val * sigmoid_val * (1.0 + gate_val * (1.0 - sigmoid_val))
    ).astype(BF)
    grad_up = (grad_hidden * activated).astype(BF)
    gate_rows = gather(grad_gate, "row")
    up_rows = gather(grad_up, "row")
    grad_residual = grad_out + scatter_sum(
        against_cols(gate_rows, gate_weight) + against_cols(up_rows, up_weight), "col"
    )
    residual_grad_block = gather(grad_residual.astype(BF), "col").astype(F32)
    mixer_gain_term = jnp.sum(grad_residual * mixer_out * mixer_scale, 0)
    mixer_stat = total(jnp.sum(grad_residual * mixer_gain_part * mixer_out, 1))
    grad_mixer = norm_backward(grad_residual, mixer_out, mixer_scale, mixer_gain_part, mixer_stat)
    grad_mixer_block = norm_backward(
        residual_grad_block, mixer_block, mixer_scale, mixer_gain_block, mixer_stat
    ).astype(BF)

    grad_attended = scatter_sum(against_cols(grad_mixer_block, output_weight), "row").astype(BF)
    grad_query_rot, grad_key_rot, grad_value = attend_backward(
        query_rot, key_rot, value_low, grad_attended, probs
    )
    grad_query_norm = rotate(grad_query_rot, cosine, -sine)
    grad_key_norm = rotate(grad_key_rot, cosine, -sine)
    query_gain_term = jnp.sum(grad_query_norm * query * query_scale, 0)
    key_gain_term = jnp.sum(grad_key_norm * key_proj * key_scale, 0)
    stats = total(
        jnp.stack(
            [
                jnp.sum(grad_query_norm * query_gain_part * query, 1),
                jnp.sum(grad_key_norm * key_gain_part * key_proj, 1),
            ]
        )
    )
    grad_query = norm_backward(
        grad_query_norm, query, query_scale, query_gain_part, stats[0]
    ).astype(BF)
    grad_key = norm_backward(
        grad_key_norm, key_proj, key_scale, key_gain_part, stats[1]
    ).astype(BF)
    grad_value_low = grad_value.astype(BF)
    query_rows = gather(grad_query, "row")
    key_rows = gather(grad_key, "row")
    value_rows = gather(grad_value_low, "row")
    grad_input = grad_residual + scatter_sum(
        against_cols(query_rows, query_weight)
        + against_cols(key_rows, key_weight)
        + against_cols(value_rows, value_weight),
        "col",
    )

    input_all = dp_share(input_block)
    residual_all = dp_share(residual_block)
    attended_all = dp_share(attended_rows)
    hidden_all = dp_share(hidden_rows)
    feed_all = gather(dp_whole(grad_feed.astype(BF)), "col")
    gate_all = gather(dp_whole(grad_gate), "row")
    up_all = gather(dp_whole(grad_up), "row")
    mixer_all = gather(dp_whole(grad_mixer.astype(BF)), "col")
    query_all = gather(dp_whole(grad_query), "row")
    key_all = gather(dp_whole(grad_key), "row")
    value_all = gather(dp_whole(grad_value_low), "row")
    gain_sums = lax.psum(
        (
            place_gain(query_gain_term, head_start),
            place_gain(key_gain_term, head_start),
            place_gain(mixer_gain_term, feature_start),
            place_gain(feed_gain_term, feature_start),
        ),
        ("dp", "row", "col"),
    )
    return (
        block_out,
        grad_input.astype(BF),
        across_rows(input_all, query_all),
        across_rows(input_all, key_all),
        across_rows(input_all, value_all),
        across_rows(attended_all, mixer_all),
        across_rows(residual_all, gate_all),
        across_rows(residual_all, up_all),
        across_rows(hidden_all, feed_all),
        *gain_sums,
    )


def solution(mesh):
    in_specs = (
        P("dp", ("row", "col")),
        P("dp"),
        P("row", "col"),
        P("row", "col"),
        P("row", "col"),
        P("col", "row"),
        P("row", "col"),
        P("row", "col"),
        P("col", "row"),
        P(),
        P(),
        P(),
        P(),
        P("dp", ("row", "col")),
    )
    out_specs = (
        P("dp", ("row", "col")),
        P("dp", ("row", "col")),
        P(("row", "dp"), "col"),
        P(("row", "dp"), "col"),
        P(("row", "dp"), "col"),
        P(("col", "dp"), "row"),
        P(("row", "dp"), "col"),
        P(("row", "dp"), "col"),
        P(("col", "dp"), "row"),
        P(),
        P(),
        P(),
        P(),
    )
    return jax.shard_map(body, mesh=mesh, in_specs=in_specs, out_specs=out_specs, check_vma=False)
```

```python
import jax
import jax.numpy as jnp
from jax import lax
from jax.sharding import PartitionSpec as P

D = 2048
HD = 128


epsilon = 1e-06
rope_base = 500000.0

BF = jnp.bfloat16
F32 = jnp.float32


def mul_f32(left, right):
    return jnp.dot(left, right, preferred_element_type=F32)


def across_rows(left, right):
    return lax.dot_general(left, right, (((0,), (0,)), ((), ())), preferred_element_type=F32)


def against_cols(left, right):
    return lax.dot_general(left, right, (((1,), (1,)), ((), ())), preferred_element_type=F32)


def swap(tensor, axis, bit):
    size = lax.axis_size(axis)
    return lax.ppermute(tensor, axis, [(i, i ^ bit) for i in range(size)])


def bits_of(axis):
    size = lax.axis_size(axis)
    bits = []
    bit = 1
    while bit < size:
        bits.append(bit)
        bit *= 2
    return bits


def ordered(pieces, axis, dim):
    me = lax.axis_index(axis)
    for bit in bits_of(axis):
        flip = (me & bit) != 0
        moved = list(pieces)
        for j in range(len(pieces)):
            if not j & bit:
                moved[j] = jnp.where(flip, pieces[j | bit], pieces[j])
                moved[j | bit] = jnp.where(flip, pieces[j], pieces[j | bit])
        pieces = moved
    return jnp.concatenate(pieces, dim)


def gather_pieces(tensor, axis, dim):
    pieces = {0: tensor}
    width = tensor.shape[dim]
    for bit in reversed(bits_of(axis)):
        keys = sorted(pieces)
        packed = jnp.concatenate([pieces[k] for k in keys], dim) if len(keys) > 1 else pieces[0]
        got = swap(packed, axis, bit)
        for place, k in enumerate(keys):
            pieces[k | bit] = lax.slice_in_dim(got, place * width, (place + 1) * width, axis=dim)
    return [pieces[j] for j in range(lax.axis_size(axis))]


def gather(tensor, axis, dim=1):
    return ordered(gather_pieces(tensor, axis, dim), axis, dim)


def share(tensor, index, width):
    return lax.dynamic_slice_in_dim(tensor, index * width, width, 1)


def scatter_sum(tensor, axis, kind=BF):
    size = lax.axis_size(axis)
    me = lax.axis_index(axis)
    width = tensor.shape[1] // size
    held = {j: share(tensor, me ^ j, width) for j in range(size)}
    for bit in bits_of(axis):
        away = [j for j in sorted(held) if j & bit]
        packed = jnp.concatenate([held[j].astype(kind) for j in away], 1)
        got = swap(packed, axis, bit)
        for place, j in enumerate(away):
            part = lax.slice_in_dim(got, place * width, (place + 1) * width, axis=1)
            held[j ^ bit] = held[j ^ bit] + part.astype(F32)
            del held[j]
    return held[0]


def total(tensor):
    for axis in ("col", "row"):
        for bit in bits_of(axis):
            tensor = tensor + swap(tensor, axis, bit)
    return tensor


def shifted(tensor, shift):
    size = lax.axis_size("dp")
    return lax.ppermute(tensor, "dp", [(i, (i + shift) % size) for i in range(size)])


def dp_share(tensors):
    size = lax.axis_size("dp")
    me = lax.axis_index("dp")
    widths = [tensor.shape[1] // size for tensor in tensors]

    def cut(index):
        return jnp.concatenate([share(t, index, w) for t, w in zip(tensors, widths)], 1)

    blocks = [cut(me)]
    for k in range(1, size):
        blocks.append(shifted(cut((me + k) % size), k))
    return blocks


def dp_spread(tensor, relay=True):
    size = lax.axis_size("dp")
    blocks = [tensor]
    if not relay or size > 4:
        for k in range(1, size):
            blocks.append(shifted(tensor, k))
        return blocks
    ups, downs = [tensor], [tensor]
    for _ in range(1, size):
        ups.append(lax.ppermute(ups[-1], "dp", [(i, i + 1) for i in range(size - 1)]))
        downs.append(lax.ppermute(downs[-1], "dp", [(i + 1, i) for i in range(size - 1)]))
    for k in range(1, size):
        blocks.append(ups[k] + downs[size - k])
    return blocks


def columns(blocks, start, width):
    return jnp.concatenate([block[:, start : start + width] for block in blocks], 0)


def two_rows(left_own, left_other, right):
    product = across_rows(left_other, right).astype(BF)
    away = swap(product, "row", 1)
    return across_rows(left_own, right), away


def placed(own, away):
    first = lax.axis_index("row") == 0
    away = away.astype(F32)
    return jnp.concatenate([jnp.where(first, own, away), jnp.where(first, away, own)], 1)


def gain_totals(terms):
    got = lax.all_gather(jnp.stack(terms), ("row", "col"))
    rows, cols = lax.axis_size("row"), lax.axis_size("col")
    got = got.reshape((rows, cols) + got.shape[1:])
    by_head = jnp.swapaxes(got, 0, 1)
    whole = jnp.stack(
        [
            by_head[:, :, 0].reshape(-1),
            by_head[:, :, 1].reshape(-1),
            got[:, :, 2].reshape(-1),
            got[:, :, 3].reshape(-1),
        ]
    )
    whole = sum(dp_spread(whole, relay=False))
    return [whole[j] for j in range(4)]


def rope_tables(row_count):
    positions = jnp.arange(row_count, dtype=F32)
    rates = rope_base ** (-2.0 * jnp.arange(HD // 2, dtype=F32) / HD)
    angles = positions[:, None] * rates[None, :]
    return (jnp.cos(angles), jnp.sin(angles))


def rotate(tensor, cosine, sine):
    half = HD // 2
    parts = []
    for start in range(0, tensor.shape[1], HD):
        first = tensor[:, start : start + half]
        second = tensor[:, start + half : start + HD]
        parts.append(first * cosine - second * sine)
        parts.append(second * cosine + first * sine)
    return jnp.concatenate(parts, 1)


def heads_of(tensor):
    return [tensor[:, s : s + HD] for s in range(0, tensor.shape[1], HD)]


def attend_forward(queries, keys, values, seq_length):
    count = queries.shape[0]
    query_pos = jnp.arange(count)[:, None]
    key_pos = jnp.arange(count)[None, :]
    allowed = (key_pos <= query_pos) & (key_pos < seq_length)
    outputs, probs = [], []
    for q, k, v in zip(heads_of(queries), heads_of(keys), heads_of(values)):
        scores = jnp.where(allowed, against_cols(q, k) * HD ** (-0.5), -1e30)
        row_max = jnp.max(scores, axis=-1, keepdims=True)
        exponent = jnp.exp(scores - row_max)
        p = exponent / jnp.sum(exponent, axis=-1, keepdims=True)
        probs.append(p)
        outputs.append(mul_f32(p.astype(BF), v))
    return jnp.concatenate(outputs, 1), probs


def attend_backward(queries, keys, values, grad_attended, probs):
    scale = HD ** (-0.5)
    gq, gk, gv = [], [], []
    for q, k, v, g, p in zip(
        heads_of(queries), heads_of(keys), heads_of(values), heads_of(grad_attended), probs
    ):
        grad_prob = against_cols(g, v)
        centre = jnp.sum(p * grad_prob, axis=-1, keepdims=True)
        grad_scores = (p * (grad_prob - centre)).astype(BF)
        gq.append(mul_f32(grad_scores, k) * scale)
        gk.append(across_rows(grad_scores, q) * scale)
        gv.append(across_rows(p.astype(BF), g))
    return jnp.concatenate(gq, 1), jnp.concatenate(gk, 1), jnp.concatenate(gv, 1)


def norm_backward(grad_norm, source, scale_rows, gain_part, stat_sum):
    weighted = grad_norm * gain_part
    return scale_rows * weighted - source * scale_rows**3 * stat_sum[:, None] / D


def layer(
    hidden_in,
    seq_lengths,
    query_weight,
    key_weight,
    value_weight,
    output_weight,
    gate_weight,
    up_weight,
    down_weight,
    query_gain,
    key_gain,
    mixer_gain,
    feed_gain,
    out_grad,
):
    row_count, width = hidden_in.shape
    row_place = lax.axis_index("row")
    col_place = lax.axis_index("col")
    col_size = lax.axis_size("col")
    feature_start = (row_place * col_size + col_place) * width
    block_start = row_place * col_size * width
    block_width = col_size * width
    head_start = (col_place * lax.axis_size("row") + row_place) * width
    query_gain_part = lax.dynamic_slice_in_dim(query_gain, head_start, width)
    key_gain_part = lax.dynamic_slice_in_dim(key_gain, head_start, width)
    mixer_gain_part = lax.dynamic_slice_in_dim(mixer_gain, feature_start, width)
    feed_gain_part = lax.dynamic_slice_in_dim(feed_gain, feature_start, width)
    mixer_gain_block = lax.dynamic_slice_in_dim(mixer_gain, block_start, block_width)
    feed_gain_block = lax.dynamic_slice_in_dim(feed_gain, block_start, block_width)
    seq_length = seq_lengths[0]
    cosine, sine = rope_tables(row_count)

    input_block = gather(hidden_in, "col")
    query_part = mul_f32(input_block, query_weight)
    key_part = mul_f32(input_block, key_weight)
    value_part = mul_f32(input_block, value_weight)
    query = scatter_sum(query_part, "row", F32)
    key_proj = scatter_sum(key_part, "row", F32)
    value_low = scatter_sum(value_part, "row").astype(BF)
    square_sums = total(jnp.stack([jnp.sum(query * query, 1), jnp.sum(key_proj * key_proj, 1)]))
    query_scale = lax.rsqrt(square_sums[0] / D + epsilon)[:, None]
    key_scale = lax.rsqrt(square_sums[1] / D + epsilon)[:, None]
    query_rot = rotate(query * query_scale * query_gain_part, cosine, sine).astype(BF)
    key_rot = rotate(key_proj * key_scale * key_gain_part, cosine, sine).astype(BF)
    attended, probs = attend_forward(query_rot, key_rot, value_low, seq_length)
    attended_rows = gather(attended.astype(BF), "row")
    mixer_out = scatter_sum(mul_f32(attended_rows, output_weight), "col")
    mixer_block = gather(mixer_out.astype(BF), "col").astype(F32)
    mixer_scale = lax.rsqrt(total(jnp.sum(mixer_out * mixer_out, 1)) / D + epsilon)[:, None]
    residual = hidden_in.astype(F32) + mixer_out * mixer_scale * mixer_gain_part
    residual_block = (
        input_block.astype(F32) + mixer_block * mixer_scale * mixer_gain_block
    ).astype(BF)

    gate_val = scatter_sum(mul_f32(residual_block, gate_weight), "row")
    up_val = scatter_sum(mul_f32(residual_block, up_weight), "row")
    sigmoid_val = jax.nn.sigmoid(gate_val)
    activated = gate_val * sigmoid_val
    hidden_low = (activated * up_val).astype(BF)
    hidden_rows = gather(hidden_low, "row")
    feed_out = scatter_sum(mul_f32(hidden_rows, down_weight), "col")
    feed_block = gather(feed_out.astype(BF), "col").astype(F32)

    valid = (jnp.arange(row_count) < seq_length)[:, None]
    grad_block = jnp.where(valid, gather(out_grad, "col").astype(F32), 0.0)
    grad_out = jnp.where(valid, out_grad.astype(F32), 0.0)
    feed_sums = total(
        jnp.stack(
            [jnp.sum(feed_out * feed_out, 1), jnp.sum(grad_out * feed_gain_part * feed_out, 1)]
        )
    )
    feed_scale = lax.rsqrt(feed_sums[0] / D + epsilon)[:, None]
    block_out = (residual + feed_out * feed_scale * feed_gain_part).astype(BF)
    feed_gain_term = jnp.sum(grad_out * feed_out * feed_scale, 0)
    grad_feed = norm_backward(grad_out, feed_out, feed_scale, feed_gain_part, feed_sums[1])
    grad_feed_block = norm_backward(
        grad_block, feed_block, feed_scale, feed_gain_block, feed_sums[1]
    ).astype(BF)

    grad_hidden = scatter_sum(against_cols(grad_feed_block, down_weight), "row")
    grad_gate = (
        grad_hidden * up_val * sigmoid_val * (1.0 + gate_val * (1.0 - sigmoid_val))
    ).astype(BF)
    grad_up = (grad_hidden * activated).astype(BF)
    gate_rows = gather(grad_gate, "row")
    up_rows = gather(grad_up, "row")
    grad_residual = grad_out + scatter_sum(
        against_cols(gate_rows, gate_weight) + against_cols(up_rows, up_weight), "col"
    )
    residual_grad_block = gather(grad_residual.astype(BF), "col").astype(F32)
    mixer_gain_term = jnp.sum(grad_residual * mixer_out * mixer_scale, 0)
    mixer_stat = total(jnp.sum(grad_residual * mixer_gain_part * mixer_out, 1))
    grad_mixer = norm_backward(grad_residual, mixer_out, mixer_scale, mixer_gain_part, mixer_stat)
    grad_mixer_block = norm_backward(
        residual_grad_block, mixer_block, mixer_scale, mixer_gain_block, mixer_stat
    ).astype(BF)

    grad_attended = scatter_sum(against_cols(grad_mixer_block, output_weight), "row").astype(BF)
    grad_query_rot, grad_key_rot, grad_value = attend_backward(
        query_rot, key_rot, value_low, grad_attended, probs
    )
    grad_query_norm = rotate(grad_query_rot, cosine, -sine)
    grad_key_norm = rotate(grad_key_rot, cosine, -sine)
    query_gain_term = jnp.sum(grad_query_norm * query * query_scale, 0)
    key_gain_term = jnp.sum(grad_key_norm * key_proj * key_scale, 0)
    stats = total(
        jnp.stack(
            [
                jnp.sum(grad_query_norm * query_gain_part * query, 1),
                jnp.sum(grad_key_norm * key_gain_part * key_proj, 1),
            ]
        )
    )
    grad_query = norm_backward(
        grad_query_norm, query, query_scale, query_gain_part, stats[0]
    ).astype(BF)
    grad_key = norm_backward(
        grad_key_norm, key_proj, key_scale, key_gain_part, stats[1]
    ).astype(BF)
    grad_value_low = grad_value.astype(BF)
    query_rows = gather(grad_query, "row")
    key_rows = gather(grad_key, "row")
    value_rows = gather(grad_value_low, "row")
    grad_input = grad_residual + scatter_sum(
        against_cols(query_rows, query_weight)
        + against_cols(key_rows, key_weight)
        + against_cols(value_rows, value_weight),
        "col",
    )

    share_width = residual_block.shape[1] // lax.axis_size("dp")
    cut = hidden_low.shape[1]
    left_blocks = dp_share([input_block, residual_block, attended_rows])
    left = columns(left_blocks, 0, 2 * share_width)
    attended_all = columns(left_blocks, 2 * share_width, left_blocks[0].shape[1] - 2 * share_width)
    other = swap(left, "row", 1)
    hidden_all = jnp.concatenate(dp_share([hidden_rows]), 0)
    feed_all = jnp.concatenate(dp_spread(grad_feed.astype(BF), relay=False), 0)
    both_blocks = dp_spread(jnp.concatenate([grad_gate, grad_up], 1))
    attention_blocks = dp_spread(
        jnp.concatenate([grad_mixer.astype(BF), grad_query, grad_key, grad_value_low], 1),
        relay=False,
    )
    mixer_all = columns(attention_blocks, 0, width)
    attention_all = columns(attention_blocks, width, 3 * width)
    feed_all = gather(feed_all, "col")
    mixer_all = gather(mixer_all, "col")
    gate_sum = placed(
        *two_rows(left[:, share_width:], other[:, share_width:], columns(both_blocks, 0, cut))
    )
    up_sum = placed(
        *two_rows(left[:, share_width:], other[:, share_width:], columns(both_blocks, cut, cut))
    )
    own, away = two_rows(left[:, :share_width], other[:, :share_width], attention_all)
    attention_sums = [
        placed(own[:, j * width : (j + 1) * width], away[:, j * width : (j + 1) * width])
        for j in range(3)
    ]
    return (
        block_out,
        grad_input.astype(BF),
        *attention_sums,
        across_rows(attended_all, mixer_all),
        gate_sum,
        up_sum,
        across_rows(hidden_all, feed_all),
        *gain_totals([query_gain_term, key_gain_term, mixer_gain_term, feed_gain_term]),
    )


def solution(mesh):
    in_specs = (
        P("dp", ("row", "col")),
        P("dp"),
        P("row", "col"),
        P("row", "col"),
        P("row", "col"),
        P("col", "row"),
        P("row", "col"),
        P("row", "col"),
        P("col", "row"),
        P(),
        P(),
        P(),
        P(),
        P("dp", ("row", "col")),
    )
    out_specs = (
        P("dp", ("row", "col")),
        P("dp", ("row", "col")),
        P(("row", "dp"), "col"),
        P(("row", "dp"), "col"),
        P(("row", "dp"), "col"),
        P(("col", "dp"), "row"),
        P(("row", "dp"), "col"),
        P(("row", "dp"), "col"),
        P(("col", "dp"), "row"),
        P(),
        P(),
        P(),
        P(),
    )
    return jax.shard_map(layer, mesh=mesh, in_specs=in_specs, out_specs=out_specs, check_vma=False)
```

```python
import jax
import jax.numpy as jnp
from jax import lax
from jax.experimental.layout import Layout, with_layout_constraint
from jax.sharding import PartitionSpec as P

D = 2048
HD = 128


epsilon = 1e-06
rope_base = 500000.0

BF = jnp.bfloat16
F32 = jnp.float32


def contract(left, right, dims):
    return lax.dot_general(left, right, (dims, ((), ())), preferred_element_type=F32)


def mul(left, right):
    return contract(left, right, ((1,), (0,)))


def across_rows(left, right):
    return contract(left, right, ((0,), (0,)))


def against_cols(left, right):
    return contract(left, right, ((1,), (1,)))


def row_major(tensor):
    return with_layout_constraint(tensor, Layout(major_to_minor=tuple(range(tensor.ndim))))


def bits_of(axis):
    size = lax.axis_size(axis)
    return [1 << j for j in range(size.bit_length() - 1)]


def swap(tensor, axis, bit):
    size = lax.axis_size(axis)
    return lax.ppermute(tensor, axis, [(i, i ^ bit) for i in range(size)])


def pieces_of(tensor, axis, dim=1):
    pieces = {0: tensor}
    width = tensor.shape[dim]
    for bit in reversed(bits_of(axis)):
        keys = sorted(pieces)
        packed = jnp.concatenate([pieces[k] for k in keys], dim) if len(keys) > 1 else pieces[0]
        got = swap(packed, axis, bit)
        for place, k in enumerate(keys):
            pieces[k | bit] = lax.slice_in_dim(got, place * width, (place + 1) * width, axis=dim)
    return [pieces[j] for j in range(lax.axis_size(axis))]


def ordered(pieces, axis, dim=1):
    me = lax.axis_index(axis)
    for bit in bits_of(axis):
        flip = (me & bit) != 0
        moved = list(pieces)
        for j in range(len(pieces)):
            if not j & bit:
                moved[j] = jnp.where(flip, pieces[j | bit], pieces[j])
                moved[j | bit] = jnp.where(flip, pieces[j], pieces[j | bit])
        pieces = moved
    return jnp.concatenate(pieces, dim)


def sum_pieces(parts, axis, kind=BF):
    held = dict(enumerate(parts))
    width = parts[0].shape[1]
    for bit in bits_of(axis):
        away = [j for j in sorted(held) if j & bit]
        packed = jnp.concatenate([held[j].astype(kind) for j in away], 1)
        got = swap(packed, axis, bit)
        for place, j in enumerate(away):
            part = lax.slice_in_dim(got, place * width, (place + 1) * width, axis=1)
            held[j ^ bit] = held[j ^ bit].astype(F32) + part.astype(F32)
            del held[j]
    return held[0]


def split_cols(tensor, width):
    return [tensor[:, s : s + width] for s in range(0, tensor.shape[1], width)]


def total(tensor):
    for axis in ("col", "row"):
        for bit in bits_of(axis):
            tensor = tensor + swap(tensor, axis, bit)
    return tensor


def dp_exchange(pieces):
    got = lax.all_to_all(jnp.stack(pieces), "dp", 0, 0, tiled=True)
    return got.reshape((len(pieces) * got.shape[1], got.shape[2]))


def dp_spread(tensor):
    return dp_exchange([tensor] * lax.axis_size("dp"))


def from_me(tensor):
    size = lax.axis_size("dp")
    me = lax.axis_index("dp")
    rows = tensor.shape[0] // size
    return jnp.concatenate(
        [
            lax.dynamic_slice_in_dim(tensor, ((me + size - k) % size) * rows, rows, 0)
            for k in range(size)
        ],
        0,
    )


def dp_relay(tensor):
    size = lax.axis_size("dp")
    if size > 4:
        return from_me(dp_spread(tensor))
    ups, downs = [tensor], [tensor]
    for _ in range(1, size):
        ups.append(lax.ppermute(ups[-1], "dp", [(i, i + 1) for i in range(size - 1)]))
        downs.append(lax.ppermute(downs[-1], "dp", [(i + 1, i) for i in range(size - 1)]))
    return jnp.concatenate([tensor] + [ups[k] + downs[size - k] for k in range(1, size)], 0)


def dp_total(tensor):
    bits = bits_of("dp")
    if len(bits) == 2:
        one, two, three = (swap(tensor, "dp", j) for j in (1, 2, 3))
        return (tensor + one) + (two + three)
    for bit in bits:
        tensor = tensor + swap(tensor, "dp", bit)
    return tensor


def row_partner(tensor):
    half = tensor.shape[0] // 2
    odd = lax.axis_index("col") % 2
    mine = swap(lax.dynamic_slice_in_dim(tensor, odd * half, half, 0), "row", 1)
    theirs = swap(mine, "col", 1)
    first = odd == 0
    return jnp.concatenate([jnp.where(first, mine, theirs), jnp.where(first, theirs, mine)], 0)


def two_rows(left_own, left_other, right):
    product = lax.optimization_barrier(across_rows(left_other, right).astype(BF))
    away = swap(product, "row", 1)
    return across_rows(left_own, right), away


def placed(own, away):
    first = lax.axis_index("row") == 0
    away = away.astype(F32)
    return jnp.concatenate([jnp.where(first, own, away), jnp.where(first, away, own)], 1)


def place_gain(term, offset):
    return lax.dynamic_update_slice_in_dim(jnp.zeros((D,), F32), term, offset, 0)


def rope_tables(row_count):
    positions = jnp.arange(row_count, dtype=F32)
    rates = rope_base ** (-2.0 * jnp.arange(HD // 2, dtype=F32) / HD)
    angles = positions[:, None] * rates[None, :]
    return (jnp.cos(angles), jnp.sin(angles))


def rotate(tensor, cosine, sine):
    half = HD // 2
    parts = []
    for start in range(0, tensor.shape[1], HD):
        first = tensor[:, start : start + half]
        second = tensor[:, start + half : start + HD]
        parts.append(first * cosine - second * sine)
        parts.append(second * cosine + first * sine)
    return jnp.concatenate(parts, 1)


def attend_forward(queries, keys, values, seq_length):
    count = queries.shape[0]
    query_pos = jnp.arange(count)[:, None]
    key_pos = jnp.arange(count)[None, :]
    allowed = (key_pos <= query_pos) & (key_pos < seq_length)
    outputs, probs = [], []
    for q, k, v in zip(split_cols(queries, HD), split_cols(keys, HD), split_cols(values, HD)):
        scores = jnp.where(allowed, against_cols(q, k) * HD ** (-0.5), -1e30)
        row_max = jnp.max(scores, axis=-1, keepdims=True)
        exponent = jnp.exp(scores - row_max)
        p = exponent / jnp.sum(exponent, axis=-1, keepdims=True)
        probs.append(p)
        outputs.append(mul(p.astype(BF), v))
    return jnp.concatenate(outputs, 1), probs


def attend_backward(queries, keys, values, grad_attended, probs):
    scale = HD ** (-0.5)
    gq, gk, gv = [], [], []
    for q, k, v, g, p in zip(
        split_cols(queries, HD),
        split_cols(keys, HD),
        split_cols(values, HD),
        split_cols(grad_attended, HD),
        probs,
    ):
        grad_prob = against_cols(g, v)
        centre = jnp.sum(p * grad_prob, axis=-1, keepdims=True)
        grad_scores = (p * (grad_prob - centre)).astype(BF)
        gq.append(mul(grad_scores, k) * scale)
        gk.append(across_rows(grad_scores, q) * scale)
        gv.append(across_rows(p.astype(BF), g))
    return jnp.concatenate(gq, 1), jnp.concatenate(gk, 1), jnp.concatenate(gv, 1)


def norm_backward(grad_norm, source, scale_rows, gain_part, stat_sum):
    weighted = grad_norm * gain_part
    return scale_rows * weighted - source * scale_rows**3 * stat_sum[:, None] / D


def layer(
    hidden_in,
    seq_lengths,
    query_weight,
    key_weight,
    value_weight,
    output_weight,
    gate_weight,
    up_weight,
    down_weight,
    query_gain,
    key_gain,
    mixer_gain,
    feed_gain,
    out_grad,
):
    row_count, width = hidden_in.shape
    row_place = lax.axis_index("row")
    col_place = lax.axis_index("col")
    col_size = lax.axis_size("col")
    row_size = lax.axis_size("row")
    dp_size = lax.axis_size("dp")
    block_width = col_size * width
    feature_start = (row_place * col_size + col_place) * width
    head_start = (col_place * row_size + row_place) * width
    half_ff = gate_weight.shape[1] // 2

    def gain_block(gain):
        return jnp.concatenate(
            [
                lax.dynamic_slice_in_dim(
                    gain, (row_place * col_size + (col_place ^ j)) * width, width
                )
                for j in range(col_size)
            ]
        )

    def rows_of(weight, half):
        cols = weight.shape[1] // 2
        blocks = [
            lax.dynamic_slice(weight, ((col_place ^ j) * width, half * cols), (width, cols))
            for j in range(col_size)
        ]
        return lax.optimization_barrier(jnp.concatenate(blocks, 0))

    def cols_of(weight, half):
        rows = weight.shape[0] // 2
        blocks = [
            lax.dynamic_slice(weight, (half * rows, (col_place ^ j) * width), (rows, width))
            for j in range(col_size)
        ]
        return lax.optimization_barrier(jnp.concatenate(blocks, 1))

    query_gain_part = lax.dynamic_slice_in_dim(query_gain, head_start, width)
    key_gain_part = lax.dynamic_slice_in_dim(key_gain, head_start, width)
    mixer_gain_part = lax.dynamic_slice_in_dim(mixer_gain, feature_start, width)
    feed_gain_part = lax.dynamic_slice_in_dim(feed_gain, feature_start, width)
    mixer_gain_block = gain_block(mixer_gain)
    feed_gain_block = gain_block(feed_gain)
    seq_length = seq_lengths[0]
    cosine, sine = rope_tables(row_count)

    out_own = cols_of(output_weight, row_place)
    out_oth = cols_of(output_weight, 1 - row_place)
    gate_own = rows_of(gate_weight, row_place)
    gate_oth = rows_of(gate_weight, 1 - row_place)
    up_own = rows_of(up_weight, row_place)
    up_oth = rows_of(up_weight, 1 - row_place)
    down_own = cols_of(down_weight, row_place)
    down_oth = cols_of(down_weight, 1 - row_place)

    input_pieces = pieces_of(hidden_in, "col")
    input_block = ordered(input_pieces, "col")

    def two_halves(tensor):
        return [
            lax.dynamic_slice_in_dim(tensor, place * width, width, 1)
            for place in (row_place, 1 - row_place)
        ]

    query = sum_pieces(two_halves(mul(input_block, query_weight)), "row", F32)
    key_proj = sum_pieces(two_halves(mul(input_block, key_weight)), "row", F32)
    value_low = sum_pieces(two_halves(mul(input_block, value_weight)), "row").astype(BF)
    square_sums = total(jnp.stack([jnp.sum(query * query, 1), jnp.sum(key_proj * key_proj, 1)]))
    query_scale = lax.rsqrt(square_sums[0] / D + epsilon)[:, None]
    key_scale = lax.rsqrt(square_sums[1] / D + epsilon)[:, None]
    query_rot = rotate(query * query_scale * query_gain_part, cosine, sine).astype(BF)
    key_rot = rotate(key_proj * key_scale * key_gain_part, cosine, sine).astype(BF)
    attended, probs = attend_forward(query_rot, key_rot, value_low, seq_length)
    attended_low = row_major(attended.astype(BF))
    attended_far = swap(attended_low, "row", 1)
    mixer_part = mul(attended_low, out_own) + mul(attended_far, out_oth)
    mixer_out = sum_pieces(split_cols(mixer_part, width), "col")
    mixer_block = jnp.concatenate(pieces_of(mixer_out.astype(BF), "col"), 1).astype(F32)
    mixer_scale = lax.rsqrt(total(jnp.sum(mixer_out * mixer_out, 1)) / D + epsilon)[:, None]
    residual = hidden_in.astype(F32) + mixer_out * mixer_scale * mixer_gain_part
    residual_block = lax.optimization_barrier(
        (
            jnp.concatenate(input_pieces, 1).astype(F32)
            + mixer_block * mixer_scale * mixer_gain_block
        ).astype(BF)
    )

    up_far = swap(mul(residual_block, up_oth).astype(BF), "row", 1)
    gate_far = swap(mul(residual_block, gate_oth).astype(BF), "row", 1)
    up_near, gate_near = lax.optimization_barrier(
        (mul(residual_block, up_own), mul(residual_block, gate_own))
    )
    up_val = up_near + up_far.astype(F32)
    gate_val = gate_near + gate_far.astype(F32)
    sigmoid_val = jax.nn.sigmoid(gate_val)
    activated = gate_val * sigmoid_val
    hidden_low = lax.optimization_barrier((activated * up_val).astype(BF))
    hidden_far = swap(hidden_low, "row", 1)
    feed_part = mul(hidden_low, down_own) + mul(hidden_far, down_oth)
    feed_out = sum_pieces(split_cols(feed_part, width), "col")
    feed_block = jnp.concatenate(pieces_of(feed_out.astype(BF), "col"), 1).astype(F32)

    valid = (jnp.arange(row_count) < seq_length)[:, None]
    out_grad_pieces = pieces_of(out_grad, "col")
    grad_block = lax.optimization_barrier(
        jnp.where(valid, jnp.concatenate(out_grad_pieces, 1).astype(F32), 0.0)
    )
    grad_out = jnp.where(valid, out_grad.astype(F32), 0.0)
    feed_sums = total(
        jnp.stack(
            [jnp.sum(feed_out * feed_out, 1), jnp.sum(grad_out * feed_gain_part * feed_out, 1)]
        ),
    )
    feed_scale = lax.rsqrt(feed_sums[0] / D + epsilon)[:, None]
    block_out = (residual + feed_out * feed_scale * feed_gain_part).astype(BF)
    feed_gain_term = jnp.sum(grad_out * feed_out * feed_scale, 0)
    grad_feed_block = lax.optimization_barrier(
        norm_backward(
            grad_block, feed_block, feed_scale, feed_gain_block, feed_sums[1]
        ).astype(BF)
    )

    grad_hidden_far = swap(against_cols(grad_feed_block, down_oth).astype(BF), "row", 1)
    grad_hidden_near = lax.optimization_barrier(against_cols(grad_feed_block, down_own))
    grad_hidden = grad_hidden_near + grad_hidden_far.astype(F32)
    grad_gate = (
        grad_hidden * up_val * sigmoid_val * (1.0 + gate_val * (1.0 - sigmoid_val))
    ).astype(BF)
    grad_up = (grad_hidden * activated).astype(BF)
    grad_gate, grad_up = lax.optimization_barrier((grad_gate, grad_up))
    gate_grad_far = swap(grad_gate, "row", 1)
    up_grad_far = swap(grad_up, "row", 1)
    grad_part = against_cols(grad_gate, gate_own) + against_cols(grad_up, up_own)
    grad_part = grad_part + against_cols(gate_grad_far, gate_oth)
    grad_part = grad_part + against_cols(up_grad_far, up_oth)
    grad_residual = grad_out + sum_pieces(split_cols(grad_part, width), "col")
    residual_grad_block = jnp.concatenate(pieces_of(grad_residual.astype(BF), "col"), 1).astype(F32)
    mixer_gain_term = jnp.sum(grad_residual * mixer_out * mixer_scale, 0)
    mixer_stat = total(jnp.sum(grad_residual * mixer_gain_part * mixer_out, 1))
    grad_mixer_block = lax.optimization_barrier(
        norm_backward(
            residual_grad_block, mixer_block, mixer_scale, mixer_gain_block, mixer_stat
        ).astype(BF)
    )

    attended_grad_far = swap(against_cols(grad_mixer_block, out_oth).astype(BF), "row", 1)
    grad_attended = (
        against_cols(grad_mixer_block, out_own) + attended_grad_far.astype(F32)
    ).astype(BF)
    grad_query_rot, grad_key_rot, grad_value = attend_backward(
        query_rot, key_rot, value_low, grad_attended, probs
    )
    grad_value_low = grad_value.astype(BF)
    grad_query_norm = rotate(grad_query_rot, cosine, -sine)
    grad_key_norm = rotate(grad_key_rot, cosine, -sine)
    query_gain_term = jnp.sum(grad_query_norm * query * query_scale, 0)
    key_gain_term = jnp.sum(grad_key_norm * key_proj * key_scale, 0)
    stats = total(
        jnp.stack(
            [
                jnp.sum(grad_query_norm * query_gain_part * query, 1),
                jnp.sum(grad_key_norm * key_gain_part * key_proj, 1),
            ]
        ),
    )
    grad_query = norm_backward(
        grad_query_norm, query, query_scale, query_gain_part, stats[0]
    ).astype(BF)
    grad_key = norm_backward(
        grad_key_norm, key_proj, key_scale, key_gain_part, stats[1]
    ).astype(BF)
    attention_grads = lax.optimization_barrier(
        jnp.concatenate([grad_query, grad_key, grad_value_low], 1)
    )
    attention_rows = ordered([attention_grads, swap(attention_grads, "row", 1)], "row")
    count = attention_grads.shape[1]

    def rows_at(place):
        return jnp.concatenate(
            [
                attention_rows[:, place * width : (place + 1) * width],
                attention_rows[:, count + place * width : count + (place + 1) * width],
            ],
            1,
        )

    input_grad_part = (
        against_cols(rows_at(0), query_weight)
        + against_cols(rows_at(1), key_weight)
        + against_cols(rows_at(2), value_weight)
    )
    grad_input = grad_residual + sum_pieces(
        [
            lax.dynamic_slice_in_dim(input_grad_part, (col_place ^ j) * width, width, 1)
            for j in range(col_size)
        ],
        "col",
    )

    gain_terms = (query_gain_term, key_gain_term, mixer_gain_term, feed_gain_term)

    share_width = block_width // dp_size
    first_row = row_place == 0

    def feature_share(block, index):
        start = index * share_width
        place = ((start // width) ^ col_place) * width + start % width
        return lax.dynamic_slice_in_dim(block, place, share_width, 1)

    def row_share(own, far, index):
        both = own.shape[1] * 2
        start = index * (both // dp_size)
        stop = start + both // dp_size
        second = start >= own.shape[1]
        start -= own.shape[1] * second
        stop -= own.shape[1] * second
        here = first_row ^ bool(second)
        return jnp.where(here, own[:, start:stop], far[:, start:stop])

    attended_rows = row_major(ordered([attended_low, attended_far], "row"))
    left_all = dp_exchange(
        [
            jnp.concatenate(
                [
                    lax.dynamic_slice_in_dim(input_block, j * share_width, share_width, 1),
                    feature_share(residual_block, j),
                    split_cols(attended_rows, attended_rows.shape[1] // dp_size)[j],
                ],
                1,
            )
            for j in range(dp_size)
        ],
    )
    left = left_all[:, : 2 * share_width]
    attended_all = left_all[:, 2 * share_width :]
    other = row_partner(left)
    hidden_all = dp_exchange([row_share(hidden_low, hidden_far, j) for j in range(dp_size)])
    feed_all = dp_spread(grad_feed_block[:, :width])
    both_all = dp_relay(jnp.concatenate([grad_gate, grad_up], 1))
    gate_all, up_all = both_all[:, :half_ff], both_all[:, half_ff:]
    mixer_all = dp_spread(grad_mixer_block[:, :width])
    attention_all = dp_spread(attention_grads)
    feed_all = ordered(pieces_of(feed_all, "col"), "col")
    mixer_all = ordered(pieces_of(mixer_all, "col"), "col")
    left_r = lax.optimization_barrier(from_me(left[:, share_width:]))
    other_r = from_me(other[:, share_width:])
    left_i, other_i = left[:, :share_width], other[:, :share_width]
    gate_sum = placed(*two_rows(left_r, other_r, gate_all))
    up_sum = placed(*two_rows(left_r, other_r, up_all))
    own, away = two_rows(left_i, other_i, attention_all)
    attention_sums = [placed(o, a) for o, a in zip(split_cols(own, width), split_cols(away, width))]

    gains = jnp.stack(
        [
            place_gain(gain_terms[0], head_start),
            place_gain(gain_terms[1], head_start),
            place_gain(gain_terms[2], feature_start),
            place_gain(gain_terms[3], feature_start),
        ]
    )
    gains = total(gains)
    gains = dp_total(gains)
    return (
        block_out,
        grad_input.astype(BF),
        *attention_sums,
        across_rows(attended_all, mixer_all),
        gate_sum,
        up_sum,
        across_rows(hidden_all, feed_all),
        *[gains[j] for j in range(4)],
    )


def solution(mesh):
    in_specs = (
        P("dp", ("row", "col")),
        P("dp"),
        P("row", "col"),
        P("row", "col"),
        P("row", "col"),
        P("col", "row"),
        P("row", "col"),
        P("row", "col"),
        P("col", "row"),
        P(),
        P(),
        P(),
        P(),
        P("dp", ("row", "col")),
    )
    out_specs = (
        P("dp", ("row", "col")),
        P("dp", ("row", "col")),
        P(("row", "dp"), "col"),
        P(("row", "dp"), "col"),
        P(("row", "dp"), "col"),
        P(("col", "dp"), "row"),
        P(("row", "dp"), "col"),
        P(("row", "dp"), "col"),
        P(("col", "dp"), "row"),
        P(),
        P(),
        P(),
        P(),
    )
    return jax.shard_map(layer, mesh=mesh, in_specs=in_specs, out_specs=out_specs, check_vma=False)
```
